32 devices in a mesh: dp: 8 (over z, x), sp: 4 (over y, core).
Axes of the slice: x: 2, y: 2, z: 4, core: 2. Of those that a mesh axis runs over, the one named last changes fastest.
Arguments:
- tokens: bfloat16 [16, 1024, 768], P('dp', 'sp'), may hold values from -6 to 6
- segment_ids: int32 [16, 1024], P('dp'), may hold values from 0 to 15, never falling along the last dimension, each value on 1 to 512 neighbouring positions
- key_mask: int32 [16, 1024], P('dp'), may hold values 0 or 1
- w_query: bfloat16 [768, 768], P('dp'), may hold values from -0.3125 to 0.3125
- b_query: bfloat16 [768], P('dp'), may hold values from -3 to 3
- w_key: bfloat16 [768, 768], P('dp'), may hold values from -0.3125 to 0.3125
- w_value: bfloat16 [768, 768], P('dp'), may hold values from -0.21875 to 0.21875
- b_value: bfloat16 [768], P('dp'), may hold values from -2 to 2
- w_attn_out: bfloat16 [768, 768], P('dp'), may hold values from -0.625 to 0.625
- b_attn_out: bfloat16 [768], P('dp'), may hold values from -2 to 2
- gain_attn: bfloat16 [768], P('dp'), may hold values from 0.5 to 1.5
- shift_attn: bfloat16 [768], P('dp'), may hold values from -2 to 2
- w_inner: bfloat16 [768, 3072], P('dp'), may hold values from -0.21875 to 0.21875
- b_inner: bfloat16 [3072], P('dp'), may hold values from -3 to 3
- w_outer: bfloat16 [3072, 768], P('dp'), may hold values from -0.15625 to 0.15625
- b_outer: bfloat16 [768], P('dp'), may hold values from -2 to 2
- gain_ffn: bfloat16 [768], P('dp'), may hold values from 0.5 to 1.5
- shift_ffn: bfloat16 [768], P('dp'), may hold values from -2 to 2
- grad_output: bfloat16 [16, 1024, 768], P('dp', 'sp'), may hold values from -6 to 6
Outputs:
- layer_out: bfloat16 [16, 1024, 768], P('dp', 'sp')
- grad_tokens: bfloat16 [16, 1024, 768], P('dp', 'sp')
- grad_w_query: float32 [768, 768], P('dp')
- grad_b_query: float32 [768], P('dp')
- grad_w_key: float32 [768, 768], P('dp')
- grad_w_value: float32 [768, 768], P('dp')
- grad_b_value: float32 [768], P('dp')
- grad_w_attn_out: float32 [768, 768], P('dp')
- grad_b_attn_out: float32 [768], P('dp')
- grad_gain_attn: float32 [768], P('dp')
- grad_shift_attn: float32 [768], P('dp')
- grad_w_inner: float32 [768, 3072], P('dp')
- grad_b_inner: float32 [3072], P('dp')
- grad_w_outer: float32 [3072, 768], P('dp')
- grad_b_outer: float32 [768], P('dp')
- grad_gain_ffn: float32 [768], P('dp')
- grad_shift_ffn: float32 [768], P('dp')
The draws below stay inside these ranges and needn't reach their ends.
Inputs may be any that keep to these rules, and one draw needn't show every extreme that they name: `segment_ids`: along each sequence the ids never fall; each id marks one document of 1 to 512 tokens, and in every sequence one document has exactly 512. `key_mask`: 0 marks a padding token, which only it itself attends to.
All inputs are finite; a program needn't handle non-finite values. No bound on the sum of `key_mask` on one device may be relied on, other than what follows from the above.
Results may differ from the reference program's by a relative error of at most 0.018.
Values may be sent and summed in bfloat16 or wider, within the bound.
A program may use at most 192 MiB of HBM per device.

```python
import math
import jax
import jax.numpy as jnp
import numpy as np
from jax import lax

D = 768
H = 12
HD = 64
FF = 3072
LEN = 1024
COUNT = 16
MOST = 512
SEQS = 16


def with_ends(result, key, smallest, top_value):
    extent = result.shape
    spot = [jax.random.randint(jax.random.fold_in(key, axis), (), 0, extent[axis]) for axis in range(len(extent))]
    result = result.at[tuple(spot)].set(smallest)
    longest = extent.index(max(extent))
    spot[longest] = (spot[longest] + 1) % extent[longest]
    return result.at[tuple(spot)].set(top_value)


def strengthened(drawn, key, source, target, parts, factor):
    def block_of(position):
        return (jnp.arange(drawn.shape[position]) // (drawn.shape[position] // parts)).reshape((-1,) + (1,) * (drawn.ndim - 1 - position))

    one_side = jax.random.permutation(key, parts)[block_of(target)]
    far = (block_of(target) + parts // 2) % parts
    return jnp.where((block_of(source) == one_side) | (block_of(source) == far), factor * drawn, drawn)


def level_of(own_key, extent, cuts, smallest, largest):
    loudness, own = 1.0, jax.random.fold_in(own_key, 6)
    for dim, parts in cuts:
        heights = jnp.exp(jax.random.uniform(jax.random.fold_in(own, dim), (parts,), jnp.float32, smallest / len(cuts), largest / len(cuts)))
        loudness = loudness * jnp.repeat(heights, extent[dim] // parts).reshape([-1 if axis == dim else 1 for axis in range(len(extent))])
    return loudness


def profile(number_of, total, bound, lean):
    portions = [(1 << 20) // math.isqrt(standing ** lean) + 1 for standing in range(2, number_of + 1)]
    surplus, given = total - bound - (number_of - 1), [1] * (number_of - 1)
    while surplus > 0:
        candidates = [i for i in range(number_of - 1) if given[i] < bound]
        whole, left = sum([portions[i] for i in candidates]), surplus
        for i in candidates:
            more = min(bound - given[i], max(1, left * portions[i] // whole), surplus)
            given[i] = given[i] + more
            surplus = surplus - more
    return np.array([bound] + given)


def uneven_parts(rng, amount, total, limit, slope):
    if amount == 2:
        one = jax.random.randint(rng, (), max(1, total - limit), min(limit, total - 1) + 1)
        return jnp.stack([one, total - one])
    tallies = jnp.asarray(profile(amount, total, limit, slope), jnp.int32)
    twos = (amount - 1) // 2
    giver, sink = tallies[1:1 + 2 * twos:2], tallies[2:2 + 2 * twos:2]
    slack = jnp.minimum(giver - 1, limit - sink)
    passed = jax.random.randint(jax.random.fold_in(rng, 1), (twos,), 0, 1 << 20) % (slack + 1)
    tallies = tallies.at[1:1 + 2 * twos:2].set(giver - passed).at[2:2 + 2 * twos:2].set(sink + passed)
    return tallies[jax.random.permutation(jax.random.fold_in(rng, 2), amount)]


def bell_draw(key, shape, deviation, limit, pieces=(), held_as=jnp.bfloat16):
    entries = jax.random.normal(key, shape, jnp.float32) * deviation
    if len(pieces) > 0:
        entries = level_of(key, shape, pieces, -0.22, 0.18) * entries
    return jnp.clip(entries, min=-limit, max=limit).astype(held_as)


def noise_with(stream_key, dims, scale, limit, split, heavy, dtype=jnp.bfloat16):
    values = scale * jax.random.normal(stream_key, dims, jnp.float32)
    if split:
        values = values * level_of(stream_key, dims, split, -0.22, 0.18)
    return jnp.clip(strengthened(values, jax.random.fold_in(stream_key, 3), *heavy), -limit, limit).astype(dtype)


def setup_inputs(seed: int = 0) -> dict:
    seeds = jax.random.split(jax.random.key(seed), 20)
    return {
        "tokens": bell_draw(seeds[0], (SEQS, LEN, D), 1.0, 6.0, ((0, 8), (1, 4))),
        "segment_ids": jax.vmap(lambda own: jnp.searchsorted(jnp.cumsum(uneven_parts(own, COUNT, LEN, MOST, 2)), jnp.arange(LEN), side="right"))(jax.random.split(seeds[1], SEQS)).reshape((SEQS, LEN)).astype(jnp.int32),
        "key_mask": with_ends((jax.random.randint(seeds[2], (SEQS, LEN), 0, 8) < 7).astype(jnp.int32), jax.random.fold_in(seeds[2], 1), 0, 1),
        "w_query": bell_draw(seeds[3], (D, D), (D // 2) ** -0.5, 0.3125, ((0, 8),)),
        "b_query": bell_draw(seeds[4], (D,), 0.5, 3.0, ((0, 8),)),
        "w_key": bell_draw(seeds[5], (D, D), (D // 2) ** -0.5, 0.3125, ((0, 8),)),
        "w_value": bell_draw(seeds[6], (D, D), D ** -0.5, 0.21875, ((0, 8),)),
        "b_value": bell_draw(seeds[7], (D,), 0.3, 2.0, ((0, 8),)),
        "w_attn_out": bell_draw(seeds[8], (D, D), (D // 8) ** -0.5, 0.625, ((0, 8),)),
        "b_attn_out": bell_draw(seeds[9], (D,), 0.3, 2.0, ((0, 8),)),
        "gain_attn": jnp.clip(1.0 + 0.1 * jax.random.normal(seeds[10], (D,), jnp.float32), 0.5, 1.5).astype(jnp.bfloat16),
        "shift_attn": bell_draw(seeds[11], (D,), 0.3, 2.0, ((0, 8),)),
        "w_inner": bell_draw(seeds[12], (D, FF), D ** -0.5, 0.21875, ((0, 8),)),
        "b_inner": bell_draw(seeds[13], (FF,), 0.5, 3.0, ((0, 8),)),
        "w_outer": bell_draw(seeds[14], (FF, D), (FF // 2) ** -0.5, 0.15625, ((0, 8),)),
        "b_outer": bell_draw(seeds[15], (D,), 0.3, 2.0, ((0, 8),)),
        "gain_ffn": jnp.clip(1.0 + 0.1 * jax.random.normal(seeds[16], (D,), jnp.float32), 0.5, 1.5).astype(jnp.bfloat16),
        "shift_ffn": bell_draw(seeds[17], (D,), 0.3, 2.0, ((0, 8),)),
        "grad_output": noise_with(seeds[18], (SEQS, LEN, D), 1.0, 6.0, ((0, 8), (1, 4)), (0, 2, 8, 2.0)),
    }


@jax.custom_vjp
def low(v):
    return lax.optimization_barrier(v.astype(jnp.bfloat16)).astype(jnp.float32)

@jax.custom_vjp
def low_back(v):
    return v

def low_keep(v):
    return (low(v), None)

def low_pass(kept, grad):
    return (grad,)

def back_keep(v):
    return (v, None)

def back_low(kept, grad):
    return (low(grad),)
low.defvjp(low_keep, low_pass)
low_back.defvjp(back_keep, back_low)
HIGHEST_PRECISION = lax.Precision.HIGHEST
EPSILON = 1e-06
MASKED_SCORE = -1e+30

def matmul(left, right):
    return jnp.dot(left, right, precision=HIGHEST_PRECISION, preferred_element_type=jnp.float32)

def normalize(summed, gain_vec, shift_vec):
    center = lax.optimization_barrier(jnp.mean(summed, axis=-1, keepdims=True))
    centered = summed - center
    spread = lax.optimization_barrier(jnp.mean(centered * centered, axis=-1, keepdims=True))
    return centered * lax.rsqrt(spread + EPSILON) * gain_vec + shift_vec

def attend(member):
    queries, keys_in, values_in, segments, keepers = member
    positions = jnp.arange(LEN)
    allowed = (segments[:, None] == segments[None, :]) & (keepers[None, :] == 1) | (positions[:, None] == positions[None, :])
    scores = jnp.einsum('qhd,khd->hqk', queries, keys_in, precision=HIGHEST_PRECISION)
    scores = low_back(scores * HD ** (-0.5))
    scores = jnp.where(allowed[None], scores, MASKED_SCORE)
    probability = low(jax.nn.softmax(scores, axis=-1))
    return jnp.einsum('hqk,khd->qhd', probability, values_in, precision=HIGHEST_PRECISION)

def layer_forward(group_in, params, segments, keepers):
    w_query, b_query, w_key, w_value, b_value, w_attn_out, b_attn_out, gain_attn, shift_attn, w_inner, b_inner, w_outer, b_outer, gain_ffn, shift_ffn = params
    token_rows = group_in.reshape(-1, D)
    queries = low_back(low(matmul(token_rows, w_query) + b_query))
    keys_all = low_back(low(matmul(token_rows, w_key)))
    values_all = low_back(low(matmul(token_rows, w_value) + b_value))
    head_shape = (group_in.shape[0], LEN, H, HD)
    attended = lax.map(jax.checkpoint(attend), (queries.reshape(head_shape), keys_all.reshape(head_shape), values_all.reshape(head_shape), segments, keepers))
    attended = low_back(low(attended.reshape(-1, D)))
    branch = low_back(matmul(attended, w_attn_out) + b_attn_out)
    hidden = normalize(token_rows + branch, gain_attn, shift_attn)
    inner = low_back(matmul(low(hidden), w_inner) + b_inner)
    active = low(jax.nn.gelu(inner, approximate=False))
    outer = low_back(matmul(active, w_outer) + b_outer)
    return normalize(hidden + outer, gain_ffn, shift_ffn).reshape(group_in.shape)

def reference(tokens, segment_ids, key_mask, w_query, b_query, w_key, w_value, b_value, w_attn_out, b_attn_out, gain_attn, shift_attn, w_inner, b_inner, w_outer, b_outer, gain_ffn, shift_ffn, grad_output):
    weights = (w_query, b_query, w_key, w_value, b_value, w_attn_out, b_attn_out, gain_attn, shift_attn, w_inner, b_inner, w_outer, b_outer, gain_ffn, shift_ffn)
    params = tuple((member.astype(jnp.float32) for member in weights))
    group_size = math.gcd(SEQS, max(1, 4096 // LEN))
    group_count = SEQS // group_size
    full_shape = (group_count, group_size, LEN, D)
    inputs = (tokens.reshape(full_shape), segment_ids.reshape(group_count, group_size, LEN), key_mask.reshape(group_count, group_size, LEN), grad_output.reshape(full_shape))
    zeroed = tuple((jnp.zeros(member.shape, jnp.float32) for member in params))

    def advance(totals, member):
        group_in, segments, keepers, cotangent = member

        def forward(inputs_f, params_f):
            return layer_forward(inputs_f, params_f, segments, keepers)
        output, pullback = jax.vjp(forward, group_in.astype(jnp.float32), params)
        grad_in, grad_params = pullback(cotangent.astype(jnp.float32))
        totals = tuple((first + second for first, second in zip(totals, grad_params)))
        return (totals, (output.astype(jnp.bfloat16), grad_in.astype(jnp.bfloat16)))
    totals, (outputs, grads_in) = lax.scan(advance, zeroed, inputs)
    g_wq, g_bq, g_wk, g_wv, g_bv, g_wo, g_bo, g_ga, g_sa, g_wi, g_bi, g_wu, g_bu, g_gf, g_sf = totals
    return (outputs.reshape(SEQS, LEN, D), grads_in.reshape(SEQS, LEN, D), g_wq, g_bq, g_wk, g_wv, g_bv, g_wo, g_bo, g_ga, g_sa, g_wi, g_bi, g_wu, g_bu, g_gf, g_sf)
```

```python
import jax
import jax.numpy as jnp
from jax import lax
from jax.experimental import pallas as pl
from jax.experimental.pallas import tpu as pltpu
from jax.sharding import PartitionSpec as P

MESH = pl.DeviceIdType.MESH
NG = 3

H = 12
HD = 64


EPSILON = 1e-06
MASKED_SCORE = -1e30


def normalize(summed, gain_vec, shift_vec):
    center = jnp.mean(summed, axis=-1, keepdims=True)
    centered = summed - center
    spread = jnp.mean(centered * centered, axis=-1, keepdims=True)
    return centered * lax.rsqrt(spread + EPSILON) * gain_vec + shift_vec


def gelu_exact(inputs_f):
    return jax.nn.gelu(inputs_f, approximate=False)


def matmul(left, right):
    return jnp.dot(left, right, preferred_element_type=jnp.float32)


def left_trans(left, right):
    return lax.dot_general(
        left, right, (((0,), (0,)), ((), ())), preferred_element_type=jnp.float32
    )


def right_trans(left, right):
    return lax.dot_general(
        left, right, (((1,), (1,)), ((), ())), preferred_element_type=jnp.float32
    )


def column_sum(values_low):
    return jnp.sum(values_low, axis=0, dtype=jnp.float32)


def score_block(query_blk, key_heads, seg_query, segments, keepers, pos_query, score_scale):
    scores = (
        jnp.einsum("qhd,khd->hqk", query_blk, key_heads, preferred_element_type=jnp.float32)
        * score_scale
    )
    positions = jnp.arange(segments.shape[0])
    allowed = (seg_query[:, None] == segments[None, :]) & (keepers[None, :] == 1) | (
        pos_query[:, None] == positions[None, :]
    )
    return jnp.where(allowed[None], scores, MASKED_SCORE)


def attend_forward(queries, keys_in, values_in, segments, keepers, head_count, score_scale):
    length = queries.shape[0]
    block_len = min(512, length)
    blocks = length // block_len
    query_heads = queries.reshape(blocks, block_len, head_count, -1)
    key_heads = keys_in.reshape(length, head_count, -1)
    value_heads = values_in.reshape(length, head_count, -1)
    seg_blocks = segments.reshape(blocks, block_len)
    pos_blocks = jnp.arange(length).reshape(blocks, block_len)

    def one_block(member):
        query_blk, seg_query, pos_query = member
        scores = score_block(
            query_blk, key_heads, seg_query, segments, keepers, pos_query, score_scale
        )
        top_score = jnp.max(scores, axis=-1, keepdims=True)
        exponent = jnp.exp(scores - top_score)
        total = jnp.sum(exponent, axis=-1, keepdims=True)
        probability = (exponent / total).astype(jnp.bfloat16)
        attended = jnp.einsum(
            "hqk,khd->qhd", probability, value_heads, preferred_element_type=jnp.float32
        )
        log_total = (top_score + jnp.log(total))[:, :, 0]
        return (attended.reshape(block_len, -1).astype(jnp.bfloat16), log_total)

    attended, log_total = lax.map(one_block, (query_heads, seg_blocks, pos_blocks))
    return (attended.reshape(length, -1), log_total)


def attend_backward(
    queries, keys_in, values_in, grad_att, log_total, segments, keepers, head_count, score_scale
):
    length = queries.shape[0]
    block_len = min(512, length)
    blocks = length // block_len
    query_heads = queries.reshape(blocks, block_len, head_count, -1)
    grad_heads = grad_att.reshape(blocks, block_len, head_count, -1)
    key_heads = keys_in.reshape(length, head_count, -1)
    value_heads = values_in.reshape(length, head_count, -1)
    seg_blocks = segments.reshape(blocks, block_len)
    pos_blocks = jnp.arange(length).reshape(blocks, block_len)

    def one_block(carry, member):
        grad_keys, grad_values = carry
        query_blk, grad_blk, total_blk, seg_query, pos_query = member
        scores = score_block(
            query_blk, key_heads, seg_query, segments, keepers, pos_query, score_scale
        )
        probability = jnp.exp(scores - total_blk[:, :, None])
        grad_prob = jnp.einsum(
            "qhd,khd->hqk", grad_blk, value_heads, preferred_element_type=jnp.float32
        )
        inner_sum = jnp.sum(probability * grad_prob, axis=-1, keepdims=True)
        grad_score = (probability * (grad_prob - inner_sum)).astype(jnp.bfloat16)
        grad_query = (
            jnp.einsum("hqk,khd->qhd", grad_score, key_heads, preferred_element_type=jnp.float32)
            * score_scale
        )
        grad_keys = (
            grad_keys
            + jnp.einsum("hqk,qhd->khd", grad_score, query_blk, preferred_element_type=jnp.float32)
            * score_scale
        )
        grad_values = grad_values + jnp.einsum(
            "hqk,qhd->khd",
            probability.astype(jnp.bfloat16),
            grad_blk,
            preferred_element_type=jnp.float32,
        )
        return ((grad_keys, grad_values), grad_query.reshape(block_len, -1).astype(jnp.bfloat16))

    zeroed = jnp.zeros(key_heads.shape, jnp.float32)
    (grad_keys, grad_values), grad_query = lax.scan(
        one_block, (zeroed, zeroed), (query_heads, grad_heads, log_total, seg_blocks, pos_blocks)
    )
    return (
        grad_query.reshape(length, -1),
        grad_keys.reshape(length, -1).astype(jnp.bfloat16),
        grad_values.reshape(length, -1).astype(jnp.bfloat16),
    )


def layer_pass(tokens, segment_ids, key_mask, shard_params, grad_output):
    (
        w_query,
        b_query,
        w_key,
        w_value,
        b_value,
        w_attn_out,
        b_attn_out,
        gain_attn,
        shift_attn,
        w_inner,
        b_inner,
        w_outer,
        b_outer,
        gain_ffn,
        shift_ffn,
    ) = shard_params
    seq_count, local_len, model_width = tokens.shape
    head_count = H // lax.axis_size("sp")
    score_scale = HD ** (-0.5)
    attn_full = (
        lax.all_gather(w_query, "dp", axis=0, tiled=True),
        lax.all_gather(b_query, "dp", axis=0, tiled=True),
        lax.all_gather(w_key, "dp", axis=0, tiled=True),
        lax.all_gather(w_value, "dp", axis=0, tiled=True),
        lax.all_gather(b_value, "dp", axis=0, tiled=True),
        lax.all_gather(w_attn_out, "dp", axis=0, tiled=True),
        lax.all_gather(b_attn_out, "dp", axis=0, tiled=True),
        lax.all_gather(gain_attn, "dp", axis=0, tiled=True),
        lax.all_gather(shift_attn, "dp", axis=0, tiled=True),
    )
    ffn_full = (
        lax.all_gather(w_inner, "dp", axis=0, tiled=True),
        lax.all_gather(b_inner, "dp", axis=0, tiled=True),
        lax.all_gather(w_outer, "dp", axis=0, tiled=True),
        lax.all_gather(b_outer, "dp", axis=0, tiled=True),
        lax.all_gather(gain_ffn, "dp", axis=0, tiled=True),
        lax.all_gather(shift_ffn, "dp", axis=0, tiled=True),
    )
    (
        full_query,
        full_bquery,
        full_key,
        full_value,
        full_bvalue,
        full_out,
        full_bout,
        full_gain1,
        full_shift1,
    ) = attn_full
    full_inner, full_binner, full_outer, full_bouter, full_gain2, full_shift2 = ffn_full
    token_rows = tokens.reshape(-1, model_width)
    local_shape = (seq_count, local_len, model_width)
    query_low = (
        (matmul(token_rows, full_query) + full_bquery).astype(jnp.bfloat16).reshape(local_shape)
    )
    keys_low = matmul(token_rows, full_key).astype(jnp.bfloat16).reshape(local_shape)
    values_low = (
        (matmul(token_rows, full_value) + full_bvalue).astype(jnp.bfloat16).reshape(local_shape)
    )
    head_query, head_keys, head_values = (
        lax.all_to_all(query_low, "sp", split_axis=2, concat_axis=1, tiled=True),
        lax.all_to_all(keys_low, "sp", split_axis=2, concat_axis=1, tiled=True),
        lax.all_to_all(values_low, "sp", split_axis=2, concat_axis=1, tiled=True),
    )

    def forward_sequence(member):
        return attend_forward(*member, head_count, score_scale)

    attended, log_total = lax.map(
        forward_sequence, (head_query, head_keys, head_values, segment_ids, key_mask)
    )
    merged = lax.all_to_all(attended, "sp", split_axis=1, concat_axis=2, tiled=True)
    merged_rows = merged.reshape(-1, model_width)
    branch = matmul(merged_rows, full_out) + full_bout
    first_sum = token_rows + branch
    hidden, attn_norm_pull = jax.vjp(
        normalize, first_sum, full_gain1.astype(jnp.float32), full_shift1.astype(jnp.float32)
    )
    hidden_low = hidden.astype(jnp.bfloat16)
    inner = matmul(hidden_low, full_inner) + full_binner
    active, gelu_pull = jax.vjp(gelu_exact, inner)
    active_low = active.astype(jnp.bfloat16)
    outer = matmul(active_low, full_outer) + full_bouter
    second_sum = hidden + outer
    result, ffn_norm_pull = jax.vjp(
        normalize, second_sum, full_gain2.astype(jnp.float32), full_shift2.astype(jnp.float32)
    )
    layer_out = result.astype(jnp.bfloat16).reshape(local_shape)
    back_inner, back_outer = (
        lax.all_gather(w_inner, "dp", axis=0, tiled=True),
        lax.all_gather(w_outer, "dp", axis=0, tiled=True),
    )
    back_query, back_key, back_value, back_out = (
        lax.all_gather(w_query, "dp", axis=0, tiled=True),
        lax.all_gather(w_key, "dp", axis=0, tiled=True),
        lax.all_gather(w_value, "dp", axis=0, tiled=True),
        lax.all_gather(w_attn_out, "dp", axis=0, tiled=True),
    )
    cotangent = grad_output.reshape(-1, model_width).astype(jnp.float32)
    grad_second, grad_gain2, grad_shift2 = ffn_norm_pull(cotangent)
    grad_outer_low = grad_second.astype(jnp.bfloat16)
    grad_bouter = column_sum(grad_outer_low)
    grad_wouter = left_trans(active_low, grad_outer_low)
    grad_active = right_trans(grad_outer_low, back_outer)
    (grad_inner,) = gelu_pull(grad_active)
    grad_inner_low = grad_inner.astype(jnp.bfloat16)
    grad_binner = column_sum(grad_inner_low)
    grad_winner = left_trans(hidden_low, grad_inner_low)
    grad_hidden = grad_second + right_trans(grad_inner_low, back_inner)
    grad_first, grad_gain1, grad_shift1 = attn_norm_pull(grad_hidden)
    grad_branch_low = grad_first.astype(jnp.bfloat16)
    grad_bout = column_sum(grad_branch_low)
    grad_wout = left_trans(merged_rows, grad_branch_low)
    grad_merged = right_trans(grad_branch_low, back_out).astype(jnp.bfloat16).reshape(local_shape)
    grad_heads = lax.all_to_all(grad_merged, "sp", split_axis=2, concat_axis=1, tiled=True)

    def backward_sequence(member):
        return attend_backward(*member, head_count, score_scale)

    head_gquery, head_gkeys, head_gvalues = lax.map(
        backward_sequence,
        (head_query, head_keys, head_values, grad_heads, log_total, segment_ids, key_mask),
    )
    grad_query, grad_keys, grad_values = (
        lax.all_to_all(head_gquery, "sp", split_axis=1, concat_axis=2, tiled=True),
        lax.all_to_all(head_gkeys, "sp", split_axis=1, concat_axis=2, tiled=True),
        lax.all_to_all(head_gvalues, "sp", split_axis=1, concat_axis=2, tiled=True),
    )
    grad_query = grad_query.reshape(-1, model_width)
    grad_keys = grad_keys.reshape(-1, model_width)
    grad_values = grad_values.reshape(-1, model_width)
    grad_wquery = left_trans(token_rows, grad_query)
    grad_bquery = column_sum(grad_query)
    grad_wkey = left_trans(token_rows, grad_keys)
    grad_wvalue = left_trans(token_rows, grad_values)
    grad_bvalue = column_sum(grad_values)
    grad_input = (
        grad_first
        + right_trans(grad_query, back_query)
        + right_trans(grad_keys, back_key)
        + right_trans(grad_values, back_value)
    )
    grad_tokens = grad_input.astype(jnp.bfloat16).reshape(local_shape)
    grads = (
        grad_wquery,
        grad_bquery,
        grad_wkey,
        grad_wvalue,
        grad_bvalue,
        grad_wout,
        grad_bout,
        grad_gain1,
        grad_shift1,
        grad_winner,
        grad_binner,
        grad_wouter,
        grad_bouter,
        grad_gain2,
        grad_shift2,
    )
    return (layer_out, grad_tokens, grads)


def body(
    tokens,
    segment_ids,
    key_mask,
    w_query,
    b_query,
    w_key,
    w_value,
    b_value,
    w_attn_out,
    b_attn_out,
    gain_attn,
    shift_attn,
    w_inner,
    b_inner,
    w_outer,
    b_outer,
    gain_ffn,
    shift_ffn,
    grad_output,
):
    shard_params = (
        w_query,
        b_query,
        w_key,
        w_value,
        b_value,
        w_attn_out,
        b_attn_out,
        gain_attn,
        shift_attn,
        w_inner,
        b_inner,
        w_outer,
        b_outer,
        gain_ffn,
        shift_ffn,
    )
    dp_count = lax.axis_size("dp")
    zeroed = tuple(
        (
            jnp.zeros((member.shape[0] * dp_count,) + member.shape[1:], jnp.float32)
            for member in shard_params
        )
    )

    def one_sequence(totals, member):
        seq_tokens, seq_segments, seq_mask, seq_grad = member
        seq_out, seq_gtok, seq_grads = layer_pass(
            seq_tokens[None], seq_segments[None], seq_mask[None], shard_params, seq_grad[None]
        )
        totals = tuple((first + second for first, second in zip(totals, seq_grads)))
        return (totals, (seq_out[0], seq_gtok[0]))

    grads, (layer_out, grad_tokens) = lax.scan(
        one_sequence, zeroed, (tokens, segment_ids, key_mask, grad_output)
    )
    g_wq, g_bq, g_wk, g_wv, g_bv, g_wo, g_bo, g_ga, g_sa, g_wi, g_bi, g_wu, g_bu, g_gf, g_sf = grads
    shards = (
        lax.psum_scatter(g_wq, "dp", scatter_dimension=0, tiled=True),
        lax.psum_scatter(g_bq, "dp", scatter_dimension=0, tiled=True),
        lax.psum_scatter(g_wk, "dp", scatter_dimension=0, tiled=True),
        lax.psum_scatter(g_wv, "dp", scatter_dimension=0, tiled=True),
        lax.psum_scatter(g_bv, "dp", scatter_dimension=0, tiled=True),
        lax.psum_scatter(g_wo, "dp", scatter_dimension=0, tiled=True),
        lax.psum_scatter(g_bo, "dp", scatter_dimension=0, tiled=True),
        lax.psum_scatter(g_ga, "dp", scatter_dimension=0, tiled=True),
        lax.psum_scatter(g_sa, "dp", scatter_dimension=0, tiled=True),
        lax.psum_scatter(g_wi, "dp", scatter_dimension=0, tiled=True),
        lax.psum_scatter(g_bi, "dp", scatter_dimension=0, tiled=True),
        lax.psum_scatter(g_wu, "dp", scatter_dimension=0, tiled=True),
        lax.psum_scatter(g_bu, "dp", scatter_dimension=0, tiled=True),
        lax.psum_scatter(g_gf, "dp", scatter_dimension=0, tiled=True),
        lax.psum_scatter(g_sf, "dp", scatter_dimension=0, tiled=True),
    )
    s_wq, s_bq, s_wk, s_wv, s_bv, s_wo, s_bo, s_ga, s_sa, s_wi, s_bi, s_wu, s_bu, s_gf, s_sf = (
        shards
    )
    summed = (
        lax.psum(s_wq.astype(jnp.bfloat16), "sp").astype(jnp.float32),
        lax.psum(s_bq.astype(jnp.bfloat16), "sp").astype(jnp.float32),
        lax.psum(s_wk.astype(jnp.bfloat16), "sp").astype(jnp.float32),
        lax.psum(s_wv.astype(jnp.bfloat16), "sp").astype(jnp.float32),
        lax.psum(s_bv.astype(jnp.bfloat16), "sp").astype(jnp.float32),
        lax.psum(s_wo.astype(jnp.bfloat16), "sp").astype(jnp.float32),
        lax.psum(s_bo.astype(jnp.bfloat16), "sp").astype(jnp.float32),
        lax.psum(s_ga.astype(jnp.bfloat16), "sp").astype(jnp.float32),
        lax.psum(s_sa.astype(jnp.bfloat16), "sp").astype(jnp.float32),
        lax.psum(s_wi.astype(jnp.bfloat16), "sp").astype(jnp.float32),
        lax.psum(s_bi.astype(jnp.bfloat16), "sp").astype(jnp.float32),
        lax.psum(s_wu.astype(jnp.bfloat16), "sp").astype(jnp.float32),
        lax.psum(s_bu.astype(jnp.bfloat16), "sp").astype(jnp.float32),
        lax.psum(s_gf.astype(jnp.bfloat16), "sp").astype(jnp.float32),
        lax.psum(s_sf.astype(jnp.bfloat16), "sp").astype(jnp.float32),
    )
    (
        out_wq,
        out_bq,
        out_wk,
        out_wv,
        out_bv,
        out_wo,
        out_bo,
        out_ga,
        out_sa,
        out_wi,
        out_bi,
        out_wu,
        out_bu,
        out_gf,
        out_sf,
    ) = summed
    return (
        layer_out,
        grad_tokens,
        out_wq,
        out_bq,
        out_wk,
        out_wv,
        out_bv,
        out_wo,
        out_bo,
        out_ga,
        out_sa,
        out_wi,
        out_bi,
        out_wu,
        out_bu,
        out_gf,
        out_sf,
    )


def coords():
    d = lax.axis_index("dp"); s = lax.axis_index("sp")
    return d // 2, d % 2, s // 2, s % 2

class AG:
    NSEM = 28
    def __init__(self, src, full, send, recv):
        self.src, self.full, self.send, self.recv = src, full, send, recv
        self.z, self.x, self.y, self.c = coords()
        self.pending = []
    def dev(self, z, x, y, c): return (z * 2 + x, y * 2 + c)
    def zp(self, dz): return lax.rem(self.z + dz, 4)
    def copy(self, src, dst, g, sslot, rslot, dev):
        cp = pltpu.make_async_remote_copy(src_ref=src, dst_ref=dst, send_sem=self.send.at[g, sslot], recv_sem=self.recv.at[g, rslot], device_id=dev, device_id_type=MESH)
        cp.start()
        self.pending.append(cp)
    def wait_recv(self, g, slot, ref):
        pltpu.make_async_remote_copy(src_ref=ref, dst_ref=ref, send_sem=self.send.at[g, slot], recv_sem=self.recv.at[g, slot], device_id=self.dev(self.z, self.x, self.y, 1 - self.c), device_id_type=MESH).wait_recv()
    def start_z(self, g):
        z, x, y, c = self.z, self.x, self.y, self.c
        q = y * 2 + c; d = z * 2 + x
        for dz in (1, 3, 2):
            zt = lax.rem(z + 4 - dz, 4)
            self.copy(self.src(g, q), self.full(g, d, q), g, dz - 1, dz - 1, self.dev(zt, x, y, c))
    def start_x(self, g):
        z, x, y, c = self.z, self.x, self.y, self.c
        d = z * 2 + x
        self.copy(self.src(g, y * 2 + c), self.full(g, d, y * 2 + c), g, 3, 3, self.dev(z, 1 - x, y, c))
        self.copy(self.src(g, (1 - y) * 2 + c), self.full(g, d, (1 - y) * 2 + c), g, 4, 7, self.dev(z, 1 - x, y, c))
    def piece(self, g, slot):
        z, x, y, c = self.z, self.x, self.y, self.c
        if slot < 3: return (self.zp(slot + 1) * 2 + x, y * 2 + c)
        if slot < 7: return (self.zp(slot - 3) * 2 + 1 - x, y * 2 + c)
        if slot == 7: return (z * 2 + 1 - x, (1 - y) * 2 + c)
        if slot < 11: return (self.zp(slot - 7) * 2 + x, (1 - y) * 2 + c)
        if slot < 14: return (self.zp(slot - 10) * 2 + 1 - x, (1 - y) * 2 + c)
        dd, qq = self.piece(g, slot - 14)
        return dd, qq + 1 - 2 * c
    def on(self, g, slot):
        z, x, y, c = self.z, self.x, self.y, self.c
        dd, qq = self.piece(g, slot)
        ref = self.full(g, dd, qq)
        self.wait_recv(g, slot, ref)
        if slot < 3:
            dz = slot + 1
            self.copy(ref, ref, g, 4 + dz, 3 + dz, self.dev(z, 1 - x, y, c))
            self.copy(ref, ref, g, 7 + dz, 7 + dz, self.dev(z, x, 1 - y, c))
        elif 4 <= slot < 7 and (slot - 3) != 2:
            dz = slot - 3
            self.copy(ref, ref, g, 10 + dz, 10 + dz, self.dev(z, x, 1 - y, c))
        elif 8 <= slot < 11 and (slot - 7) == 2:
            dz = slot - 7
            self.copy(ref, ref, g, 10 + dz, 10 + dz, self.dev(z, 1 - x, y, c))
        if slot < 14:
            self.copy(ref, ref, g, 14 + slot, 14 + slot, self.dev(z, x, y, 1 - c))
    def finish(self):
        for cp in self.pending: cp.wait_send()

def barrier(peers):
    b = pltpu.get_barrier_semaphore()
    for p in peers: pl.semaphore_signal(b, inc=1, device_id=p, device_id_type=MESH)
    pl.semaphore_wait(b, len(peers))

def ag_kernel(wq, wk, wv, wo, wi, wu, f0, f1, f2, send, recv, lsem):
    def full(g, d, q):
        if g == 0: return f0.at[q, pl.ds(pl.multiple_of(d * 96, 96), 96), :]
        if g == 1: return f1.at[q, pl.ds(pl.multiple_of(d * 96, 96), 96), :]
        return f2.at[pl.ds(pl.multiple_of(d * 384 + q * 96, 96), 96), :]
    z, x, y, c = coords()
    d = z * 2 + x
    loc = []
    for q, w in enumerate((wq, wk, wv, wo)):
        loc.append(pltpu.make_async_copy(w, full(0, d, q), lsem.at[q]))
        loc.append(pltpu.make_async_copy(wi.at[:, pl.ds(q * 768, 768)], full(1, d, q), lsem.at[4 + q]))
        loc.append(pltpu.make_async_copy(wu.at[pl.ds(q * 96, 96), :], full(2, d, q), lsem.at[8 + q]))
    def src(g, q):
        return full(g, d, q)
    ag = AG(src, full, send, recv)
    barrier([ag.dev(ag.zp(1), x, y, c), ag.dev(ag.zp(2), x, y, c), ag.dev(ag.zp(3), x, y, c), ag.dev(z, 1 - x, y, c), ag.dev(z, x, 1 - y, c), ag.dev(z, x, y, 1 - c)])
    for l in loc: l.start()
    for l in loc: l.wait()
    ag.start_z(0); ag.start_x(0)
    for g in range(NG):
        for slot in (0, 2, 1): ag.on(g, slot)
        if g + 1 < NG: ag.start_z(g + 1); ag.start_x(g + 1)
        for slot in (3, 7, 4, 8, 6, 10, 5, 9): ag.on(g, slot)
        for slot in (11, 13, 12): ag.on(g, slot)
    for g in range(NG):
        for slot in range(14, 28): ag.on(g, slot)
    ag.finish()

def ag_call(wq, wk, wv, wo, wi, wu, space=pl.ANY):
    bf = jnp.bfloat16
    return pl.pallas_call(
        ag_kernel,
        out_shape=[jax.ShapeDtypeStruct((4, 768, 768), bf), jax.ShapeDtypeStruct((4, 768, 768), bf), jax.ShapeDtypeStruct((3072, 768), bf)],
        in_specs=[pl.BlockSpec(memory_space=pl.ANY)] * 6,
        out_specs=[pl.BlockSpec(memory_space=space)] * 3,
        scratch_shapes=[pltpu.SemaphoreType.DMA((NG, 28)), pltpu.SemaphoreType.DMA((NG, 28)), pltpu.SemaphoreType.DMA((12,))],
        compiler_params=pltpu.CompilerParams(collective_id=0, has_side_effects=True),
    )(wq, wk, wv, wo, wi, wu)

A, B, C, D = 0, 1, 2, 3
SE, SD, SB, SC_, SZ, SFY, SFC = 0, 16, 20, 24, 28, 31, 32
NS = 34

class RS:
    def __init__(self, grad, S, E, Dr, Br, Cr, Zr, acc, fin, send, recv):
        self.grad = grad; self.S=S; self.E=E; self.Dr=Dr; self.Br=Br; self.Cr=Cr; self.Zr=Zr; self.acc=acc; self.fin=fin
        self.send=send; self.recv=recv
        self.z,self.x,self.y,self.c = coords()
        self.pending=[]
    def dev(self, z,x,y,c): return (z*2+x, y*2+c)
    def zp(self, dz): return lax.rem(self.z+dz,4)
    def xfirst(self, g, dz): return dz in ((0,1,3) if g % 2 == 0 else (0, 2))
    def piece(self, role, dz, c):
        x = self.x if role in (A, C) else 1 - self.x
        y = self.y if role in (A, B) else 1 - self.y
        return self.zp(dz)*2 + x, y*2 + c
    def copy(self, src, dst, g, slot, dev):
        cp = pltpu.make_async_remote_copy(src_ref=src, dst_ref=dst, send_sem=self.send.at[g, slot], recv_sem=self.recv.at[g, slot], device_id=dev, device_id_type=MESH)
        cp.start(); self.pending.append(cp)
    def wait(self, g, slot, ref):
        pltpu.make_async_remote_copy(src_ref=ref, dst_ref=ref, send_sem=self.send.at[g, slot], recv_sem=self.recv.at[g, slot], device_id=self.dev(self.z,self.x,self.y,1-self.c), device_id_type=MESH).wait_recv()
    def nx(self): return self.dev(self.z,1-self.x,self.y,self.c)
    def ny(self): return self.dev(self.z,self.x,1-self.y,self.c)
    def nc(self): return self.dev(self.z,self.x,self.y,1-self.c)
    def start(self, g):
        for role in (D, B, C, A):
            for dz in (1,2,3,0):
                d,q = self.piece(role, dz, 1-self.c)
                self.copy(self.grad(g,d,q), self.E.at[g, role*4+dz], g, SE+role*4+dz, self.nc())
    def add(self, dst, refs, f32=False):
        def step(i, _):
            r = pl.ds(pl.multiple_of(i*32,32),32)
            t = refs[0][r,:].astype(jnp.float32)
            for a in refs[1:]: t = t + a[r,:].astype(jnp.float32)
            dst[r,:] = t.astype(dst.dtype)
            return 0
        lax.fori_loop(0,3,step,0)
    def mine(self, g, role, dz):
        d,q = self.piece(role, dz, self.c)
        i = role*4+dz
        self.wait(g, SE+i, self.E.at[g,i])
        return [self.grad(g,d,q), self.E.at[g,i]]
    def diag(self, g, dz):
        i = D*4+dz
        self.add(self.S.at[g,i], self.mine(g,D,dz))
        self.copy(self.S.at[g,i], self.Dr.at[g,dz], g, SD+dz, self.nx() if self.xfirst(g,dz) else self.ny())
    def bsend(self, g, dz):
        i = B*4+dz
        refs = self.mine(g,B,dz)
        if not self.xfirst(g,dz):
            self.wait(g, SD+dz, self.Dr.at[g,dz]); refs.append(self.Dr.at[g,dz])
        self.add(self.S.at[g,i], refs)
        self.copy(self.S.at[g,i], self.Br.at[g,dz], g, SB+dz, self.nx())
    def csend(self, g, dz):
        i = C*4+dz
        refs = self.mine(g,C,dz)
        if self.xfirst(g,dz):
            self.wait(g, SD+dz, self.Dr.at[g,dz]); refs.append(self.Dr.at[g,dz])
        self.add(self.S.at[g,i], refs)
        self.copy(self.S.at[g,i], self.Cr.at[g,dz], g, SC_+dz, self.ny())
    def asend(self, g, dz):
        i = A*4+dz
        refs = self.mine(g,A,dz)
        self.wait(g, SB+dz, self.Br.at[g,dz]); self.wait(g, SC_+dz, self.Cr.at[g,dz])
        refs += [self.Br.at[g,dz], self.Cr.at[g,dz]]
        if dz == 0:
            self.add(self.acc.at[g], refs)
        else:
            self.add(self.S.at[g,i], refs)
            self.copy(self.S.at[g,i], self.Zr.at[g,3-dz], g, SZ+3-dz, self.dev(self.zp(dz),self.x,self.y,self.c))
    def total(self, g):
        refs=[self.acc.at[g]]
        for k in range(3):
            self.wait(g, SZ+k, self.Zr.at[g,k]); refs.append(self.Zr.at[g,k])
        q = self.y*2+self.c
        f = self.fin.at[g,q]
        self.add(f, refs)
        self.copy(f, f, g, SFY, self.ny())
        self.copy(f, f, g, SFC, self.nc())
    def fwd(self, g):
        f = self.fin.at[g,(1-self.y)*2+self.c]
        self.wait(g, SFY, f)
        self.copy(f, f, g, SFC+1, self.nc())
    def last(self, g):
        self.wait(g, SFC, self.fin.at[g, self.y*2+1-self.c])
        self.wait(g, SFC+1, self.fin.at[g, (1-self.y)*2+1-self.c])
    def finish(self):
        for cp in self.pending: cp.wait_send()

def rs_kernel(g0, g1, g2, oq, ok, ov, oo, oi, ou, S, E, Dr, Br, Cr, Zr, acc, fin, send, recv):
    def grad(g,d,q):
        if g == 0: return g0.at[q, pl.ds(pl.multiple_of(d*96,96),96), :]
        if g == 1: return g1.at[q, pl.ds(pl.multiple_of(d*96,96),96), :]
        return g2.at[pl.ds(pl.multiple_of(d*384+q*96,96),96), :]
    rs = RS(grad,S,E,Dr,Br,Cr,Zr,acc,fin,send,recv)
    barrier([rs.nx(), rs.ny(), rs.nc()] + [rs.dev(rs.zp(k),rs.x,rs.y,rs.c) for k in (1,2,3)])
    order = (2, 1, 0)
    for g in order: rs.start(g)
    for g in order:
        for dz in (1,2,3,0): rs.diag(g,dz)
        for dz in (1,2,3,0):
            if rs.xfirst(g,dz): rs.bsend(g,dz)
            else: rs.csend(g,dz)
        for dz in (1,2,3,0):
            if rs.xfirst(g,dz): rs.csend(g,dz)
            else: rs.bsend(g,dz)
        if g != 2:
            for dz in (1,2,3,0): rs.asend(g+1,dz)
    for dz in (1,2,3,0): rs.asend(0,dz)
    for g in order: rs.total(g)
    for g in order: rs.fwd(g)
    for g in order: rs.last(g)
    def out(o, g, q, lanes=None, rows=None):
        def step(i,_):
            r = pl.ds(pl.multiple_of(i*32,32),32)
            v = fin[g,q,r,:].astype(jnp.float32)
            if lanes is not None: o[r, lanes:lanes+768] = v
            else: o[pl.ds(pl.multiple_of(rows+i*32,32),32),:] = v
            return 0
        lax.fori_loop(0,3,step,0)
    for q,o in enumerate((oq,ok,ov,oo)): out(o,0,q,rows=0)
    for q in range(4): out(oi,1,q,lanes=q*768)
    for q in range(4): out(ou,2,q,rows=q*96)
    rs.finish()

def rs_call(g0,g1,g2):
    bf=jnp.bfloat16; f=jnp.float32
    V=pltpu.VMEM
    return pl.pallas_call(
        rs_kernel,
        out_shape=[jax.ShapeDtypeStruct((96,768),f)]*4+[jax.ShapeDtypeStruct((96,3072),f), jax.ShapeDtypeStruct((384,768),f)],
        in_specs=[pl.BlockSpec(memory_space=pltpu.VMEM)]*3,
        out_specs=[pl.BlockSpec(memory_space=pltpu.VMEM)]*6,
        scratch_shapes=[V((NG,16,96,768),bf),V((NG,16,96,768),bf),V((NG,4,96,768),bf),V((NG,4,96,768),bf),V((NG,4,96,768),bf),V((NG,3,96,768),bf),V((NG,96,768),f),V((NG,4,96,768),bf),
            pltpu.SemaphoreType.DMA((NG,NS)), pltpu.SemaphoreType.DMA((NG,NS))],
        compiler_params=pltpu.CompilerParams(collective_id=1, has_side_effects=True, vmem_limit_bytes=60<<20),
    )(g0,g1,g2)

def fast_body(tokens, segment_ids, key_mask, w_query, b_query, w_key, w_value, b_value, w_attn_out, b_attn_out, gain_attn,
              shift_attn, w_inner, b_inner, w_outer, b_outer, gain_ffn, shift_ffn, grad_output):
    f32, bf16 = jnp.float32, jnp.bfloat16
    seq_count, local_len, width = tokens.shape
    head_count = H // lax.axis_size("sp")
    score_scale = HD ** (-0.5)
    a0, a1, a2 = ag_call(w_query, w_key, w_value, w_attn_out, w_inner, w_outer)
    wq, wk, wv, wo = a0[0], a0[1], a0[2], a0[3]
    small = jnp.concatenate([jnp.stack([b_query, b_value, b_attn_out, gain_attn, shift_attn, b_outer, gain_ffn, shift_ffn]),
                             b_inner.reshape(4, 96)])
    smalls = lax.all_gather(small, "dp", axis=0)
    vec = lambda i: smalls[:, i].reshape(-1)
    bq, bv, bo, ga, sa, bu, gf, sf = [vec(i) for i in range(8)]
    bi = smalls[:, 8:12].reshape(-1)
    rows = tokens.reshape(-1, width)
    shape3 = (seq_count, local_len, width)
    a2h = lambda t: lax.all_to_all(t.reshape(shape3), "sp", split_axis=2, concat_axis=1, tiled=True)
    a2t = lambda t: lax.all_to_all(t, "sp", split_axis=1, concat_axis=2, tiled=True).reshape(-1, width)
    query = a2h((matmul(rows, wq) + bq).astype(bf16))
    keys = a2h(matmul(rows, wk).astype(bf16))
    values = a2h((matmul(rows, wv) + bv).astype(bf16))
    attended, log_total = lax.map(lambda m: attend_forward(*m, head_count, score_scale), (query, keys, values, segment_ids, key_mask))
    merged = a2t(attended)
    first_sum = rows + (matmul(merged, wo) + bo)
    hidden, pull1 = jax.vjp(normalize, first_sum, ga.astype(f32), sa.astype(f32))
    hidden_low = hidden.astype(bf16)
    inner = jnp.concatenate([matmul(hidden_low, a1[i]) for i in range(4)], axis=1) + bi
    active, gpull = jax.vjp(gelu_exact, inner)
    active_low = active.astype(bf16)
    second = hidden + (matmul(active_low, a2) + bu)
    result, pull2 = jax.vjp(normalize, second, gf.astype(f32), sf.astype(f32))
    layer_out = result.astype(bf16).reshape(shape3)
    grad_second, g_gf, g_sf = pull2(grad_output.reshape(-1, width).astype(f32))
    gol = grad_second.astype(bf16)
    g_bu = column_sum(gol)
    g_wu = left_trans(active_low, gol).astype(bf16)
    (grad_inner,) = gpull(right_trans(gol, a2))
    gil = grad_inner.astype(bf16)
    g_bi = column_sum(gil)
    g_wi = jnp.stack([left_trans(hidden_low, gil[:, i * 768:(i + 1) * 768]).astype(bf16) for i in range(4)])
    back = sum(right_trans(gil[:, i * 768:(i + 1) * 768], a1[i]) for i in range(4))
    grad_first, g_ga, g_sa = pull1(grad_second + back)
    gbl = grad_first.astype(bf16)
    g_bo = column_sum(gbl)
    g_wo = left_trans(merged, gbl).astype(bf16)
    gheads = a2h(right_trans(gbl, wo).astype(bf16))
    hq, hk, hv = lax.map(lambda m: attend_backward(*m, head_count, score_scale),
                         (query, keys, values, gheads, log_total, segment_ids, key_mask))
    gq, gk, gv = a2t(hq), a2t(hk), a2t(hv)
    g_w0 = jnp.stack([left_trans(rows, gq).astype(bf16), left_trans(rows, gk).astype(bf16), left_trans(rows, gv).astype(bf16), g_wo])
    g_bq, g_bv = column_sum(gq), column_sum(gv)
    grad_tokens = (grad_first + right_trans(gq, wq) + right_trans(gk, wk) + right_trans(gv, wv)).astype(bf16).reshape(shape3)
    oq, ok, ov, oo, oi, ou = rs_call(g_w0, g_wi, g_wu)
    vecs = jnp.stack([g_bq, g_bv, g_bo, g_ga, g_sa, g_bu, g_gf, g_sf])
    vecs = jnp.concatenate([vecs, g_bi.reshape(4, 768)])
    vecs = lax.psum(vecs, ("dp", "sp"))
    d = lax.axis_index("dp")
    cut = lax.dynamic_slice(vecs[:8], (0, d * 96), (8, 96))
    s_bi = lax.dynamic_slice(vecs[8:].reshape(-1), (d * 384,), (384,))
    return (layer_out, grad_tokens, oq, cut[0], ok, ov, cut[1], oo, cut[2], cut[3], cut[4], oi, s_bi, ou, cut[5], cut[6], cut[7])


def solution(mesh):
    return jax.shard_map(
        fast_body if mesh.shape['dp'] == 8 and mesh.shape['sp'] == 4 else body,
        mesh=mesh,
        in_specs=(
            P("dp", "sp", None),
            P("dp", None),
            P("dp", None),
            P("dp", None),
            P("dp"),
            P("dp", None),
            P("dp", None),
            P("dp"),
            P("dp", None),
            P("dp"),
            P("dp"),
            P("dp"),
            P("dp", None),
            P("dp"),
            P("dp", None),
            P("dp"),
            P("dp"),
            P("dp"),
            P("dp", "sp", None),
        ),
        out_specs=(
            P("dp", "sp", None),
            P("dp", "sp", None),
            P("dp", None),
            P("dp"),
            P("dp", None),
            P("dp", None),
            P("dp"),
            P("dp", None),
            P("dp"),
            P("dp"),
            P("dp"),
            P("dp", None),
            P("dp"),
            P("dp", None),
            P("dp"),
            P("dp"),
            P("dp"),
        ),
        check_vma=False,
    )
```
